32 devices in a mesh: grp: 4 (over x, core), dev: 8 (over z, y).
Axes of the slice: x: 2, y: 2, z: 4, core: 2. Of those that a mesh axis runs over, the one named last changes fastest.
Arguments:
- tables: float32 [4, 65536, 128], P(None, ('grp', 'dev')), may hold values from -6 to 6
- accum: float32 [4, 65536], P(None, ('grp', 'dev')), may hold values from 0.01 to 10
- block_position: int32 [4, 512], replicated, may hold values from 0 to 511, as said below
- lookup_ids: int32 [8192, 4], P(('grp', 'dev')), may hold values from 0 to 65535, as said below
Outputs:
- new_tables: float32 [4, 65536, 128], P('grp', 'dev')
- new_accum: float32 [4, 65536], P('grp', 'dev')
- looked: float32 [8192, 4, 128], P(('grp', 'dev'))
The draws below stay inside these ranges and needn't reach their ends.
Inputs may be any that keep to these rules, and one draw needn't show every extreme that they name: `block_position`: for each table a permutation of 0 to 511. Old block b lies on the device b // 16 of grp+dev; call its dev index its source, and p // 64 the owner of new block p. For every table, source and owner, at most 9 blocks of that source go to that owner, and 9 is reached. `lookup_ids`: the owner of an id of table t is block_position[t, id // 128] // 64. Among one device's 256 rows, at most 64 ids of one table have one owner, and 64 is reached for every device and table.
All inputs are finite; a program needn't handle non-finite values.
Results may differ from the reference program's by a relative error of at most 0.00002.
Values sent between devices are 32-bit elements; how exact they have to be, the bound alone decides.
A program may use at most 128 MiB of HBM per device.

```python
import math
import jax
import jax.numpy as jnp

DIM = 128
TILE = 128
BLK_DEV = 64
LOOK_DEV = 256
TABLES = 4
ROWS = 65536
N_GRP = 4
N_DEV = 8


def band_counts(key_first, key_second, length):
    starts = jax.random.permutation(key_first, N_DEV)
    shifts = jax.random.permutation(key_second, N_DEV)
    offset = (shifts[None, :] - starts[:, None]) % N_DEV
    return jnp.maximum((length - 1 - offset) // N_DEV + 1, 0).astype(jnp.int32)


def positions_table(table_key):
    keys = jax.random.split(table_key, 6)
    longer = BLK_DEV // 2 + 1
    counts = band_counts(keys[0], keys[1], longer) + band_counts(keys[2], keys[3], BLK_DEV - longer)
    owners = jnp.arange(N_DEV, dtype=jnp.int32)
    targets = jax.vmap(lambda count: jnp.repeat(owners, count, total_repeat_length=BLK_DEV))(counts)
    source_keys = jax.random.split(keys[4], N_DEV)
    shuffled = jax.vmap(lambda one_key, line: jax.random.permutation(one_key, line))(source_keys, targets)
    flat = shuffled.reshape(-1).astype(jnp.int32)
    total = N_DEV * BLK_DEV
    breaker = jax.random.permutation(keys[5], total).astype(jnp.int32)
    ordering = jnp.argsort(flat * total + breaker, stable=True)
    placed = jnp.zeros((total,), jnp.int32).at[ordering].set(jnp.arange(total, dtype=jnp.int32))
    per_old = placed.reshape(N_DEV, N_GRP, BLK_DEV // N_GRP).transpose(1, 0, 2)
    return per_old.reshape(-1)


def make_positions(key):
    base = jax.random.fold_in(key, 11)
    table_keys = jax.vmap(lambda number: jax.random.fold_in(base, number))(jnp.arange(N_GRP))
    return jax.vmap(positions_table)(table_keys)


def draw_block_position(key, part):
    return make_positions(key).astype(jnp.int32)


def draw_lookup_ids(key, part):
    positions = make_positions(key)
    inverse = jnp.argsort(positions, axis=1).astype(jnp.int32)
    base = jax.random.fold_in(key, 23)
    limit = 2 * LOOK_DEV // N_DEV

    def one_block(device, table):
        block_key = jax.random.fold_in(jax.random.fold_in(base, device), table)
        keys = jax.random.split(block_key, 5)
        chosen = jax.random.randint(keys[0], (), 0, N_DEV)
        others = jax.random.permutation(keys[1], (N_DEV - 1) * limit)[:LOOK_DEV - limit] // limit
        others = others + (others >= chosen).astype(others.dtype)
        owner_list = jnp.concatenate([jnp.full((limit,), chosen, jnp.int32), others.astype(jnp.int32)])
        owner_list = jax.random.permutation(keys[2], owner_list)
        within = jax.random.randint(keys[3], (LOOK_DEV,), 0, BLK_DEV)
        offset = jax.random.randint(keys[4], (LOOK_DEV,), 0, TILE)
        inverse_row = inverse[table]
        return inverse_row[owner_list * BLK_DEV + within] * TILE + offset
    devices = jnp.arange(N_GRP * N_DEV)
    tables_list = jnp.arange(N_GRP)
    drawn = jax.vmap(lambda device: jax.vmap(lambda table: one_block(device, table))(tables_list))(devices)
    return drawn.transpose(0, 2, 1).reshape(N_GRP * N_DEV * LOOK_DEV, N_GRP).astype(jnp.int32)


def level_of(key, extent, cuts, smallest, largest):
    gain, own = 1.0, jax.random.fold_in(key, 6)
    for axis_at, parts in cuts:
        steps = jnp.exp(jax.random.uniform(jax.random.fold_in(own, axis_at), (parts,), jnp.float32, smallest / len(cuts), largest / len(cuts)))
        gain = gain * jnp.repeat(steps, extent[axis_at] // parts).reshape([-1 if axis == axis_at else 1 for axis in range(len(extent))])
    return gain


def scatter_about(key, shape, scale, most, cuts=(), held_as=jnp.bfloat16):
    values = jax.random.normal(key, shape, jnp.float32) * scale
    if len(cuts) > 0:
        values = level_of(key, shape, cuts, -0.22, 0.18) * values
    return jnp.clip(values, min=-most, max=most).astype(held_as)


def setup_inputs(seed: int = 0) -> dict:
    key_list = jax.random.split(jax.random.key(seed), 5)
    tables = scatter_about(key_list[0], (TABLES, ROWS, DIM), 1.0, 6.0, ((1, 32),), jnp.float32)
    accum = jnp.clip(jnp.exp(math.log(10.0) - 6.9077553 * jax.random.uniform(key_list[1], (TABLES, ROWS), jnp.float32) ** level_of(key_list[1], (TABLES, ROWS), ((1, 32),), -0.2, 0.2)), 0.01, 10.0)
    block_position = draw_block_position(jax.random.fold_in(key_list[4], 71), 0)
    lookup_ids = draw_lookup_ids(jax.random.fold_in(key_list[4], 71), 0)
    return dict(tables=tables, accum=accum, block_position=block_position, lookup_ids=lookup_ids)


def reference(tables, accum, block_position, lookup_ids):
    table_count, row_count, width = tables.shape
    block_count = block_position.shape[1]
    tile_rows = row_count // block_count
    inverse = jnp.argsort(block_position, axis=1).astype(jnp.int32)
    blocks = tables.reshape(table_count, block_count, tile_rows, width)
    moved = jnp.take_along_axis(blocks, inverse[:, :, None, None], axis=1)
    new_tables = moved.reshape(table_count, row_count, width)
    sums = accum.reshape(table_count, block_count, tile_rows)
    new_accum = jnp.take_along_axis(sums, inverse[:, :, None], axis=1).reshape(table_count, row_count)
    which = jnp.arange(table_count, dtype=jnp.int32)[None, :]
    looked = tables[which, lookup_ids]
    return new_tables, new_accum, looked
```

```python
import functools

import jax
import jax.numpy as jnp
from jax import lax
from jax.experimental import pallas as pl
from jax.experimental.pallas import tpu as pltpu
from jax.sharding import PartitionSpec as P

TILE = 128
CHUNKS = 4
MESH = pl.DeviceIdType.MESH


def kernel(groups, shards, capacity, limit, *refs):
    source_of, picker, final, tables, sums, asking = refs[:6]
    new_table, new_sums, looked = refs[6:9]
    held = refs[9 : 9 + CHUNKS]
    send = refs[9 + CHUNKS : 9 + 2 * CHUNKS]
    got = refs[9 + 2 * CHUNKS : 9 + 3 * CHUNKS]
    (
        held_sums,
        send_sums,
        got_sums,
        table,
        asked,
        asked_scalar,
        answer,
        returned,
        grp_send,
        grp_recv,
        dev_send,
        dev_recv,
        ask_sem,
        ans_sem,
        own_grp,
        own_dev,
        own_sem,
        out_sem,
    ) = refs[9 + 3 * CHUNKS :]
    my_group = lax.axis_index("grp")
    my_shard = lax.axis_index("dev")
    devices = groups * shards
    me = my_group * shards + my_shard
    per_old = tables.shape[1]
    tile_rows = tables.shape[2]
    piece = tile_rows // CHUNKS
    local = groups * per_old
    slots = shards * capacity

    def coords(peer):
        return (peer // shards, peer % shards)

    def remote(src, dst, send_sem, recv_sem, device):
        return pltpu.make_async_remote_copy(
            src_ref=src,
            dst_ref=dst,
            send_sem=send_sem,
            recv_sem=recv_sem,
            device_id=device,
            device_id_type=MESH,
        )

    barrier = pltpu.get_barrier_semaphore()

    def greet(step, carry):
        pl.semaphore_signal(
            barrier, inc=1, device_id=coords((me + step) % devices), device_id_type=MESH
        )
        return carry

    lax.fori_loop(1, devices, greet, 0)
    pl.semaphore_wait(barrier, devices - 1)

    mine = pl.ds(my_group * per_old, per_old)
    own_copies = []
    for chunk in range(CHUNKS):
        rows = pl.ds(chunk * piece, piece)
        for step in range(1, groups):
            wanted = (my_group + step) % groups
            remote(
                tables.at[wanted, :, rows, :],
                held[chunk].at[mine],
                grp_send.at[chunk],
                grp_recv.at[chunk],
                (wanted, my_shard),
            ).start()
        own = pltpu.make_async_copy(
            tables.at[my_group, :, rows, :], held[chunk].at[mine], own_grp.at[chunk]
        )
        own.start()
        own_copies.append(own)
        if chunk == 0:
            for step in range(1, groups):
                wanted = (my_group + step) % groups
                remote(
                    sums.at[wanted],
                    held_sums.at[mine],
                    grp_send.at[CHUNKS],
                    grp_recv.at[CHUNKS],
                    (wanted, my_shard),
                ).start()
            own_sums_copy = pltpu.make_async_copy(
                sums.at[my_group], held_sums.at[mine], own_grp.at[CHUNKS]
            )
            own_sums_copy.start()

    def ask(step, carry):
        peer = (me + step) % devices
        remote(
            asking.at[peer], asked.at[me], ask_sem.at[0], ask_sem.at[1], coords(peer)
        ).start()
        return carry

    lax.fori_loop(1, devices, ask, 0)
    own_ask = pltpu.make_async_copy(asking.at[me], asked.at[me], own_sem.at[0])
    own_ask.start()

    order = sorted(range(1, shards), key=lambda step: abs(step - shards // 2))
    others = pl.ds(0, (groups - 1) * per_old)
    other_slots = pl.ds(0, (shards - 1) * capacity)
    own_dev_copies = []

    def exchange(send_ref, got_ref, index):
        for step in order:
            peer = (my_shard + step) % shards
            remote(
                send_ref.at[pl.ds(peer * capacity, capacity)],
                got_ref.at[pl.ds(my_shard * capacity, capacity)],
                dev_send.at[index],
                dev_recv.at[index],
                (my_group, peer),
            ).start()
        own = pltpu.make_async_copy(
            send_ref.at[pl.ds(my_shard * capacity, capacity)],
            got_ref.at[pl.ds(my_shard * capacity, capacity)],
            own_dev.at[index],
        )
        own.start()
        own_dev_copies.append(own)

    for chunk in range(CHUNKS):
        own_copies[chunk].wait()
        remote(
            held[chunk].at[others],
            held[chunk].at[others],
            grp_send.at[chunk],
            grp_recv.at[chunk],
            (my_group, my_shard),
        ).wait_recv()

        def pack(slot, carry):
            send[chunk][slot] = held[chunk][source_of[slot]]
            return carry

        lax.fori_loop(0, slots, pack, 0)
        exchange(send[chunk], got[chunk], chunk)
        if chunk == 0:
            own_sums_copy.wait()
            remote(
                held_sums.at[others],
                held_sums.at[others],
                grp_send.at[CHUNKS],
                grp_recv.at[CHUNKS],
                (my_group, my_shard),
            ).wait_recv()

            def pack_sums(slot, carry):
                send_sums[slot] = held_sums[source_of[slot]]
                return carry

            lax.fori_loop(0, slots, pack_sums, 0)
            exchange(send_sums, got_sums, CHUNKS)

    own_ask.wait()
    remote(
        asked.at[pl.ds(0, devices - 1)],
        asked.at[pl.ds(0, devices - 1)],
        ask_sem.at[0],
        ask_sem.at[1],
        (my_group, my_shard),
    ).wait_recv()
    to_scalar = pltpu.make_async_copy(asked, asked_scalar, own_sem.at[1])
    to_scalar.start()
    to_scalar.wait()

    def arrived(got_ref, index):
        own_dev_copies[index].wait()
        remote(
            got_ref.at[other_slots],
            got_ref.at[other_slots],
            dev_send.at[index],
            dev_recv.at[index],
            (my_group, my_shard),
        ).wait_recv()

    own_dev_copies[:] = [own_dev_copies[0]] + own_dev_copies[2:] + [own_dev_copies[1]]

    arrived(got_sums, CHUNKS)

    def place_sums(place, carry):
        new_sums[place] = got_sums[picker[place]]
        return carry

    lax.fori_loop(0, local, place_sums, 0)

    for chunk in range(CHUNKS):
        arrived(got[chunk], chunk)

        def place_rows(place, carry):
            start = pl.multiple_of(place * tile_rows + chunk * piece, piece)
            table[pl.ds(start, piece), :] = got[chunk][picker[place]]
            return carry

        lax.fori_loop(0, local, place_rows, 0)

    out = pltpu.make_async_copy(table, new_table, out_sem)
    out.start()

    def gather(peer):
        for at in range(limit):
            row = asked_scalar[peer, 0, at]
            answer[peer, at : at + 1, :] = table[pl.ds(row, 1), :]

    def reply(step, carry):
        peer = (me + devices // 2 + step) % devices

        @pl.when(peer != me)
        def _():
            gather(peer)
            remote(
                answer.at[peer], returned.at[me], ans_sem.at[0], ans_sem.at[1], coords(peer)
            ).start()

        return carry

    lax.fori_loop(0, devices, reply, 0)
    gather(me)
    own_answer = pltpu.make_async_copy(answer.at[me], returned.at[me], own_sem.at[2])
    own_answer.start()
    own_answer.wait()
    remote(
        returned.at[pl.ds(0, devices - 1)],
        returned.at[pl.ds(0, devices - 1)],
        ans_sem.at[0],
        ans_sem.at[1],
        (my_group, my_shard),
    ).wait_recv()

    batch = 16

    def look(step, carry):
        for at in range(batch):
            index = final[step * batch + at]
            looked[pl.ds(step * batch + at, 1), :] = returned[
                index // limit, pl.ds(index % limit, 1), :
            ]
        return carry

    lax.fori_loop(0, looked.shape[0] // batch, look, 0)

    for chunk in range(CHUNKS):
        remote(
            held[chunk].at[others],
            held[chunk].at[others],
            grp_send.at[chunk],
            grp_recv.at[chunk],
            (my_group, my_shard),
        ).wait_send()
        remote(
            send[chunk].at[other_slots],
            send[chunk].at[other_slots],
            dev_send.at[chunk],
            dev_recv.at[chunk],
            (my_group, my_shard),
        ).wait_send()
    remote(
        held_sums.at[others],
        held_sums.at[others],
        grp_send.at[CHUNKS],
        grp_recv.at[CHUNKS],
        (my_group, my_shard),
    ).wait_send()
    remote(
        send_sums.at[other_slots],
        send_sums.at[other_slots],
        dev_send.at[CHUNKS],
        dev_recv.at[CHUNKS],
        (my_group, my_shard),
    ).wait_send()
    for ref, sem in ((asked, ask_sem), (returned, ans_sem)):
        remote(
            ref.at[pl.ds(0, devices - 1)],
            ref.at[pl.ds(0, devices - 1)],
            sem.at[0],
            sem.at[1],
            (my_group, my_shard),
        ).wait_send()
    out.wait()


def body(tables, accum, block_position, lookup_ids):
    groups = lax.axis_size("grp")
    shards = lax.axis_size("dev")
    my_group = lax.axis_index("grp")
    my_shard = lax.axis_index("dev")
    table_count, old_rows, width = tables.shape
    per_old = old_rows // TILE
    local = groups * per_old
    longer = local // 2 + 1
    capacity = -(-longer // shards) + -(-(local - longer) // shards)
    look_rows = lookup_ids.shape[0]
    limit = 2 * look_rows // shards
    devices = groups * shards
    i32 = jnp.int32

    position_row = lax.dynamic_index_in_dim(block_position, my_group, 0, keepdims=False)
    by_source = position_row.reshape(groups, shards, per_old)
    places = lax.dynamic_index_in_dim(by_source, my_shard, 1, keepdims=False).reshape(-1)
    target = places // local
    counter = jnp.arange(local, dtype=i32)
    before = (target[:, None] == target[None, :]) & (counter[:, None] < counter[None, :])
    slot_of = target * capacity + jnp.sum(before.astype(i32), axis=0)
    slot = jnp.arange(shards * capacity, dtype=i32)
    source_of = jnp.sum(jnp.where(slot_of[:, None] == slot[None, :], counter[:, None], 0), axis=0)

    old = jnp.arange(position_row.shape[0], dtype=i32)
    place = my_shard * local + counter
    inverse = jnp.sum(jnp.where(position_row[None, :] == place[:, None], old[None, :], 0), axis=1)
    source = inverse // per_old % shards
    rank = inverse // (per_old * shards) * per_old + inverse % per_old
    ahead = (source[:, None] == source[None, :]) & (rank[:, None] < rank[None, :])
    picker = source * capacity + jnp.sum(ahead.astype(i32), axis=0)

    ids = lookup_ids.T
    block_of = ids // TILE
    id_place = jnp.sum(
        jnp.where(block_of[:, None, :] == old[None, :, None], block_position[:, :, None], 0), axis=1
    )
    owner = id_place // local
    local_row = id_place % local * TILE + ids % TILE
    at = jnp.arange(look_rows, dtype=i32)
    earlier = (owner[:, :, None] == owner[:, None, :]) & (at[:, None] < at[None, :])[None]
    seat = owner * limit + jnp.sum(earlier.astype(i32), axis=1)
    seats = jnp.arange(shards * limit, dtype=i32)
    asking = jnp.sum(
        jnp.where(seat[:, :, None] == seats[None, None, :], local_row[:, :, None], 0), axis=1
    )
    asking = asking.reshape(devices, 1, limit)
    lanes = -(-limit // 128) * 128
    asking = jnp.pad(asking, ((0, 0), (0, 0), (0, lanes - limit)))
    final = (jnp.arange(table_count, dtype=i32)[:, None] * (shards * limit) + seat).T.reshape(-1)

    piece = TILE // CHUNKS
    f32 = jnp.float32
    vmem = pl.BlockSpec(memory_space=pltpu.VMEM)
    smem = pl.BlockSpec(memory_space=pltpu.SMEM)
    hbm = pl.BlockSpec(memory_space=pl.ANY)
    new_table, new_sums, looked = pl.pallas_call(
        functools.partial(kernel, groups, shards, capacity, limit),
        out_shape=(
            jax.ShapeDtypeStruct((local * TILE, width), f32),
            jax.ShapeDtypeStruct((local, 1, TILE), f32),
            jax.ShapeDtypeStruct((look_rows * table_count, width), f32),
        ),
        in_specs=[smem, smem, smem, hbm, vmem, vmem],
        out_specs=(hbm, vmem, vmem),
        scratch_shapes=[pltpu.VMEM((local, piece, width), f32) for _ in range(CHUNKS)]
        + [pltpu.VMEM((shards * capacity, piece, width), f32) for _ in range(2 * CHUNKS)]
        + [
            pltpu.VMEM((local, 1, TILE), f32),
            pltpu.VMEM((shards * capacity, 1, TILE), f32),
            pltpu.VMEM((shards * capacity, 1, TILE), f32),
            pltpu.VMEM((local * TILE, width), f32),
            pltpu.VMEM((devices, 1, lanes), i32),
            pltpu.SMEM((devices, 1, lanes), i32),
            pltpu.VMEM((devices, limit, width), f32),
            pltpu.VMEM((devices, limit, width), f32),
            pltpu.SemaphoreType.DMA((CHUNKS + 1,)),
            pltpu.SemaphoreType.DMA((CHUNKS + 1,)),
            pltpu.SemaphoreType.DMA((CHUNKS + 1,)),
            pltpu.SemaphoreType.DMA((CHUNKS + 1,)),
            pltpu.SemaphoreType.DMA((2,)),
            pltpu.SemaphoreType.DMA((2,)),
            pltpu.SemaphoreType.DMA((CHUNKS + 1,)),
            pltpu.SemaphoreType.DMA((CHUNKS + 1,)),
            pltpu.SemaphoreType.DMA((3,)),
            pltpu.SemaphoreType.DMA,
        ],
        compiler_params=pltpu.CompilerParams(
            collective_id=0, has_side_effects=True, vmem_limit_bytes=60 * 1024 * 1024
        ),
    )(
        source_of,
        picker,
        final,
        tables.reshape(table_count, per_old, TILE, width),
        accum.reshape(table_count, per_old, 1, TILE),
        asking,
    )
    return (
        new_table.reshape(1, local * TILE, width),
        new_sums.reshape(1, local * TILE),
        looked.reshape(look_rows, table_count, width),
    )


def solution(mesh):
    placed = (P(None, ("grp", "dev"), None), P(None, ("grp", "dev")), P(), P(("grp", "dev"), None))
    return jax.shard_map(
        body,
        mesh=mesh,
        in_specs=placed,
        out_specs=(P("grp", "dev", None), P("grp", "dev"), P(("grp", "dev"), None, None)),
        check_vma=False,
    )
```

```python
import functools

import jax
import jax.numpy as jnp
from jax import lax
from jax.experimental import pallas as pl
from jax.experimental.pallas import tpu as pltpu
from jax.sharding import PartitionSpec as P

TILE = 128
CHUNKS = 8
LANES = 128
SPAN = 512
MESH = pl.DeviceIdType.MESH


def iota(shape, axis):
    return lax.broadcasted_iota(jnp.int32, shape, axis)


def as_row(column, lanes):
    shape = (column.shape[0], lanes)
    return jnp.sum(
        jnp.where(iota(shape, 0) == iota(shape, 1), column, 0), axis=0, keepdims=True
    )


def kernel(groups, shards, capacity, limit, *refs):
    positions, ids, tables, accum = refs[:4]
    table, new_sums, looked = refs[4:7]
    held = refs[7 : 7 + CHUNKS]
    send = refs[7 + CHUNKS : 7 + 2 * CHUNKS]
    got = refs[7 + 2 * CHUNKS : 7 + 3 * CHUNKS]
    (
        held_sums,
        send_sums,
        got_sums,
        sums,
        source_words,
        picker_words,
        final_words,
        source_of,
        picker,
        final,
        asking,
        asked,
        asked_scalar,
        answer,
        returned,
        grp_send,
        grp_recv,
        dev_send,
        dev_recv,
        ask_sem,
        ans_sem,
        own_grp,
        own_dev,
        own_sem,
        word_sem,
    ) = refs[7 + 3 * CHUNKS :]
    my_group = lax.axis_index("grp")
    my_shard = lax.axis_index("dev")
    devices = groups * shards
    me = my_group * shards + my_shard
    per_old = tables.shape[1]
    tile_rows = tables.shape[2]
    piece = tile_rows // CHUNKS
    local = groups * per_old
    slots = shards * capacity
    table_count, block_count = positions.shape
    look_rows = ids.shape[0]

    def prepare_source():
        number = iota((local, 1), 0)
        place = jnp.zeros((local, 1), jnp.int32)
        for base in range(0, block_count, SPAN):
            span = min(SPAN, block_count - base)
            old = base + iota((local, span), 1)
            counter = old // (per_old * shards) * per_old + old % per_old
            match = (old // per_old % shards == my_shard) & (counter == number)
            row = positions[pl.ds(my_group, 1), base : base + span]
            place += jnp.sum(jnp.where(match, row, 0), axis=1, keepdims=True)
        target = place // local
        lane, line = iota((local, local), 1), iota((local, local), 0)
        before = (target == as_row(target, local)) & (lane < line)
        slot_of = target * capacity + jnp.sum(jnp.where(before, 1, 0), axis=1, keepdims=True)
        slot = iota((local, source_words.shape[1]), 1)
        source_words[...] = jnp.sum(jnp.where(slot_of == slot, number, 0), axis=0, keepdims=True)
        copy = pltpu.make_async_copy(source_words, source_of, word_sem.at[0])
        copy.start()
        copy.wait()

    def prepare_picker():
        place = my_shard * local + iota((local, 1), 0)
        inverse = jnp.zeros((local, 1), jnp.int32)
        for base in range(0, block_count, SPAN):
            span = min(SPAN, block_count - base)
            old = base + iota((local, span), 1)
            row = positions[pl.ds(my_group, 1), base : base + span]
            inverse += jnp.sum(jnp.where(row == place, old, 0), axis=1, keepdims=True)
        source = inverse // per_old % shards
        rank = inverse // (per_old * shards) * per_old + inverse % per_old
        ahead = (as_row(source, local) == source) & (as_row(rank, local) < rank)
        pick = source * capacity + jnp.sum(jnp.where(ahead, 1, 0), axis=1, keepdims=True)
        picker_words[...] = as_row(pick, picker_words.shape[1])
        copy = pltpu.make_async_copy(picker_words, picker, word_sem.at[1])
        copy.start()
        copy.wait()

    def prepare_requests(index):
        wanted = ids[:, index : index + 1]
        block = wanted // tile_rows
        place = jnp.zeros((look_rows, 1), jnp.int32)
        for base in range(0, block_count, SPAN):
            span = min(SPAN, block_count - base)
            row = positions[index : index + 1, base : base + span]
            match = block == base + iota((look_rows, span), 1)
            place += jnp.sum(jnp.where(match, row, 0), axis=1, keepdims=True)
        owner = place // local
        local_row = place % local * tile_rows + wanted % tile_rows
        lane, line = iota((look_rows, look_rows), 1), iota((look_rows, look_rows), 0)
        before = (owner == as_row(owner, look_rows)) & (lane < line)
        turn = jnp.sum(jnp.where(before, 1, 0), axis=1, keepdims=True)
        seat = (index * shards + owner) * limit + turn
        final_words[index : index + 1, :] = as_row(seat, look_rows)

        def list_rows(shard, carry):
            match = (owner == shard) & (turn == iota((look_rows, asking.shape[2]), 1))
            asking[index * shards + shard] = jnp.sum(
                jnp.where(match, local_row, 0), axis=0, keepdims=True
            )
            return carry

        lax.fori_loop(0, shards, list_rows, 0)

    def coords(peer):
        return (peer // shards, peer % shards)

    def remote(src, dst, send_sem, recv_sem, device):
        return pltpu.make_async_remote_copy(
            src_ref=src,
            dst_ref=dst,
            send_sem=send_sem,
            recv_sem=recv_sem,
            device_id=device,
            device_id_type=MESH,
        )

    for index in range(table_count):
        for block in range(per_old):
            sums[index, block] = accum[index : index + 1, block * tile_rows : (block + 1) * tile_rows]

    barrier = pltpu.get_barrier_semaphore()

    def greet(step, carry):
        pl.semaphore_signal(
            barrier, inc=1, device_id=coords((me + step) % devices), device_id_type=MESH
        )
        return carry

    lax.fori_loop(1, devices, greet, 0)
    pl.semaphore_wait(barrier, devices - 1)

    mine = pl.ds(my_group * per_old, per_old)
    own_copies = []
    for chunk in range(CHUNKS):
        rows = pl.ds(chunk * piece, piece)
        for step in range(1, groups):
            wanted = (my_group + step) % groups
            remote(
                tables.at[wanted, :, rows, :],
                held[chunk].at[mine],
                grp_send.at[chunk],
                grp_recv.at[chunk],
                (wanted, my_shard),
            ).start()
        own = pltpu.make_async_copy(
            tables.at[my_group, :, rows, :], held[chunk].at[mine], own_grp.at[chunk]
        )
        own.start()
        own_copies.append(own)
        if chunk == 0:
            for step in range(1, groups):
                wanted = (my_group + step) % groups
                remote(
                    sums.at[wanted],
                    held_sums.at[mine],
                    grp_send.at[CHUNKS],
                    grp_recv.at[CHUNKS],
                    (wanted, my_shard),
                ).start()
            own_sums_copy = pltpu.make_async_copy(
                sums.at[my_group], held_sums.at[mine], own_grp.at[CHUNKS]
            )
            own_sums_copy.start()

    order = sorted(range(1, shards), key=lambda step: abs(step - shards // 2))
    others = pl.ds(0, (groups - 1) * per_old)
    other_slots = pl.ds(0, (shards - 1) * capacity)
    own_dev_copies = []

    def exchange(send_ref, got_ref, index):
        for step in order:
            peer = (my_shard + step) % shards
            remote(
                send_ref.at[pl.ds(peer * capacity, capacity)],
                got_ref.at[pl.ds(my_shard * capacity, capacity)],
                dev_send.at[index],
                dev_recv.at[index],
                (my_group, peer),
            ).start()
        own = pltpu.make_async_copy(
            send_ref.at[pl.ds(my_shard * capacity, capacity)],
            got_ref.at[pl.ds(my_shard * capacity, capacity)],
            own_dev.at[index],
        )
        own.start()
        own_dev_copies.append(own)

    def send_requests():
        def ask(step, carry):
            peer = (me + step) % devices
            remote(
                asking.at[peer], asked.at[me], ask_sem.at[0], ask_sem.at[1], coords(peer)
            ).start()
            return carry

        lax.fori_loop(1, devices, ask, 0)
        own_ask = pltpu.make_async_copy(asking.at[me], asked.at[me], own_sem.at[0])
        own_ask.start()
        return own_ask

    prepare_source()
    for chunk in range(CHUNKS):
        own_copies[chunk].wait()
        remote(
            held[chunk].at[others],
            held[chunk].at[others],
            grp_send.at[chunk],
            grp_recv.at[chunk],
            (my_group, my_shard),
        ).wait_recv()

        def pack(slot, carry):
            send[chunk][slot] = held[chunk][source_of[0, slot]]
            return carry

        lax.fori_loop(0, slots, pack, 0)
        exchange(send[chunk], got[chunk], chunk)
        if chunk == 0:
            own_sums_copy.wait()
            remote(
                held_sums.at[others],
                held_sums.at[others],
                grp_send.at[CHUNKS],
                grp_recv.at[CHUNKS],
                (my_group, my_shard),
            ).wait_recv()

            def pack_sums(slot, carry):
                send_sums[slot] = held_sums[source_of[0, slot]]
                return carry

            lax.fori_loop(0, slots, pack_sums, 0)
            exchange(send_sums, got_sums, CHUNKS)
        if chunk < table_count:
            prepare_requests(chunk)
        if chunk == min(table_count, CHUNKS) - 1:
            for index in range(chunk + 1, table_count):
                prepare_requests(index)
            own_ask = send_requests()

    prepare_picker()
    final_copy = pltpu.make_async_copy(final_words, final, word_sem.at[2])
    final_copy.start()
    final_copy.wait()

    own_ask.wait()
    remote(
        asked.at[pl.ds(0, devices - 1)],
        asked.at[pl.ds(0, devices - 1)],
        ask_sem.at[0],
        ask_sem.at[1],
        (my_group, my_shard),
    ).wait_recv()
    to_scalar = pltpu.make_async_copy(asked, asked_scalar, own_sem.at[1])
    to_scalar.start()
    to_scalar.wait()

    def arrived(got_ref, index):
        own_dev_copies[index].wait()
        remote(
            got_ref.at[other_slots],
            got_ref.at[other_slots],
            dev_send.at[index],
            dev_recv.at[index],
            (my_group, my_shard),
        ).wait_recv()

    own_dev_copies[:] = [own_dev_copies[0]] + own_dev_copies[2:] + [own_dev_copies[1]]

    arrived(got_sums, CHUNKS)

    def place_sums(place, carry):
        new_sums[place] = got_sums[picker[0, place]]
        return carry

    lax.fori_loop(0, local, place_sums, 0)

    for chunk in range(CHUNKS):
        arrived(got[chunk], chunk)

        def place_rows(place, carry):
            start = pl.multiple_of(place * tile_rows + chunk * piece, piece)
            table[pl.ds(start, piece), :] = got[chunk][picker[0, place]]
            return carry

        lax.fori_loop(0, local, place_rows, 0)

    def gather(peer):
        for at in range(limit):
            row = asked_scalar[peer, 0, at]
            answer[peer, at : at + 1, :] = table[pl.ds(row, 1), :]

    def reply(step, carry):
        turn = step // groups
        sign = turn % 2
        away = shards // 2 + sign * (turn + 1) // 2 - (1 - sign) * (turn // 2)
        group = (my_group + groups - 1 - step % groups) % groups
        shard = (my_shard + away) % shards
        peer = group * shards + shard
        gather(peer)
        remote(
            answer.at[peer],
            returned.at[pl.ds(me * limit, limit)],
            ans_sem.at[0],
            ans_sem.at[1],
            (group, shard),
        ).start()
        return carry

    lax.fori_loop(0, devices - 1, reply, 0)
    gather(me)
    own_answer = pltpu.make_async_copy(
        answer.at[me], returned.at[pl.ds(me * limit, limit)], own_sem.at[2]
    )
    own_answer.start()
    own_answer.wait()
    remote(
        returned.at[pl.ds(0, (devices - 1) * limit)],
        returned.at[pl.ds(0, (devices - 1) * limit)],
        ans_sem.at[0],
        ans_sem.at[1],
        (my_group, my_shard),
    ).wait_recv()

    batch = 16 // table_count

    def look(step, carry):
        for at in range(batch):
            for index in range(table_count):
                line = (step * batch + at) * table_count + index
                seat = final[index, step * batch + at]
                looked[pl.ds(line, 1), :] = returned[pl.ds(seat, 1), :]
        return carry

    lax.fori_loop(0, look_rows // batch, look, 0)

    for chunk in range(CHUNKS):
        remote(
            held[chunk].at[others],
            held[chunk].at[others],
            grp_send.at[chunk],
            grp_recv.at[chunk],
            (my_group, my_shard),
        ).wait_send()
        remote(
            send[chunk].at[other_slots],
            send[chunk].at[other_slots],
            dev_send.at[chunk],
            dev_recv.at[chunk],
            (my_group, my_shard),
        ).wait_send()
    remote(
        held_sums.at[others],
        held_sums.at[others],
        grp_send.at[CHUNKS],
        grp_recv.at[CHUNKS],
        (my_group, my_shard),
    ).wait_send()
    remote(
        send_sums.at[other_slots],
        send_sums.at[other_slots],
        dev_send.at[CHUNKS],
        dev_recv.at[CHUNKS],
        (my_group, my_shard),
    ).wait_send()
    for ref, sem, count in ((asked, ask_sem, 1), (returned, ans_sem, limit)):
        remote(
            ref.at[pl.ds(0, (devices - 1) * count)],
            ref.at[pl.ds(0, (devices - 1) * count)],
            sem.at[0],
            sem.at[1],
            (my_group, my_shard),
        ).wait_send()


def body(tables, accum, block_position, lookup_ids):
    groups = lax.axis_size("grp")
    shards = lax.axis_size("dev")
    table_count, old_rows, width = tables.shape
    per_old = old_rows // TILE
    local = groups * per_old
    longer = local // 2 + 1
    capacity = -(-longer // shards) + -(-(local - longer) // shards)
    look_rows = lookup_ids.shape[0]
    limit = 2 * look_rows // shards
    devices = groups * shards
    i32 = jnp.int32
    lanes = -(-limit // LANES) * LANES
    words = -(-shards * capacity // LANES) * LANES
    local_lanes = -(-local // LANES) * LANES
    piece = TILE // CHUNKS
    f32 = jnp.float32
    vmem = pl.BlockSpec(memory_space=pltpu.VMEM)
    hbm = pl.BlockSpec(memory_space=pl.ANY)
    new_table, new_sums, looked = pl.pallas_call(
        functools.partial(kernel, groups, shards, capacity, limit),
        out_shape=(
            jax.ShapeDtypeStruct((local * TILE, width), f32),
            jax.ShapeDtypeStruct((local, 1, TILE), f32),
            jax.ShapeDtypeStruct((look_rows * table_count, width), f32),
        ),
        in_specs=[vmem, vmem, hbm, vmem],
        out_specs=(vmem, vmem, vmem),
        scratch_shapes=[pltpu.VMEM((local, piece, width), f32) for _ in range(CHUNKS)]
        + [pltpu.VMEM((shards * capacity, piece, width), f32) for _ in range(2 * CHUNKS)]
        + [
            pltpu.VMEM((local, 1, TILE), f32),
            pltpu.VMEM((shards * capacity, 1, TILE), f32),
            pltpu.VMEM((shards * capacity, 1, TILE), f32),
            pltpu.VMEM((table_count, per_old, 1, TILE), f32),
            pltpu.VMEM((1, words), i32),
            pltpu.VMEM((1, local_lanes), i32),
            pltpu.VMEM((table_count, look_rows), i32),
            pltpu.SMEM((1, words), i32),
            pltpu.SMEM((1, local_lanes), i32),
            pltpu.SMEM((table_count, look_rows), i32),
            pltpu.VMEM((devices, 1, lanes), i32),
            pltpu.VMEM((devices, 1, lanes), i32),
            pltpu.SMEM((devices, 1, lanes), i32),
            pltpu.VMEM((devices, limit, width), f32),
            pltpu.VMEM((devices * limit, width), f32),
            pltpu.SemaphoreType.DMA((CHUNKS + 1,)),
            pltpu.SemaphoreType.DMA((CHUNKS + 1,)),
            pltpu.SemaphoreType.DMA((CHUNKS + 1,)),
            pltpu.SemaphoreType.DMA((CHUNKS + 1,)),
            pltpu.SemaphoreType.DMA((2,)),
            pltpu.SemaphoreType.DMA((2,)),
            pltpu.SemaphoreType.DMA((CHUNKS + 1,)),
            pltpu.SemaphoreType.DMA((CHUNKS + 1,)),
            pltpu.SemaphoreType.DMA((3,)),
            pltpu.SemaphoreType.DMA((3,)),
        ],
        compiler_params=pltpu.CompilerParams(
            collective_id=0, has_side_effects=True, vmem_limit_bytes=60 * 1024 * 1024
        ),
    )(
        block_position,
        lookup_ids,
        tables.reshape(table_count, per_old, TILE, width),
        accum,
    )
    return (
        new_table.reshape(1, local * TILE, width),
        new_sums.reshape(1, local * TILE),
        looked.reshape(look_rows, table_count, width),
    )


def solution(mesh):
    placed = (P(None, ("grp", "dev"), None), P(None, ("grp", "dev")), P(), P(("grp", "dev"), None))
    return jax.shard_map(
        body,
        mesh=mesh,
        in_specs=placed,
        out_specs=(P("grp", "dev", None), P("grp", "dev"), P(("grp", "dev"), None, None)),
        check_vma=False,
    )
```

```python
import functools

import jax
import jax.numpy as jnp
from jax import lax
from jax.experimental import pallas as pl
from jax.experimental.pallas import tpu as pltpu
from jax.sharding import PartitionSpec as P

TILE = 128
PIECES = (8, 8, 16, 16, 16, 16, 16, 16, 16)
STARTS = tuple(sum(PIECES[:index]) for index in range(len(PIECES)))
CHUNKS = len(PIECES)
LANES = 128
SPAN = 512
UNROLL = 8
MESH = pl.DeviceIdType.MESH


def iota(shape, axis):
    return lax.broadcasted_iota(jnp.int32, shape, axis)


def as_row(column, lanes):
    shape = (column.shape[0], lanes)
    return jnp.sum(
        jnp.where(iota(shape, 0) == iota(shape, 1), column, 0), axis=0, keepdims=True
    )


def as_column(row):
    shape = (row.shape[1], row.shape[1])
    return jnp.sum(jnp.where(iota(shape, 0) == iota(shape, 1), row, 0), axis=1, keepdims=True)


def kernel(groups, shards, capacity, limit, *refs):
    positions_hbm, ids_hbm, tables, accum_hbm = refs[:4]
    table, new_sums, looked = refs[4:7]
    held = refs[7 : 7 + CHUNKS]
    send = refs[7 + CHUNKS : 7 + 2 * CHUNKS]
    got = refs[7 + 2 * CHUNKS : 7 + 3 * CHUNKS]
    (
        held_sums,
        send_sums,
        got_sums,
        positions,
        ids,
        accum,
        sums,
        source_words,
        picker_words,
        final_words,
        source_of,
        picker,
        final,
        asking,
        asked,
        asked_scalar,
        answer,
        returned,
        grp_send,
        grp_recv,
        dev_send,
        dev_recv,
        ask_sem,
        ans_sem,
        own_grp,
        own_dev,
        own_sem,
        word_sem,
        load_sem,
    ) = refs[7 + 3 * CHUNKS :]
    my_group = lax.axis_index("grp")
    my_shard = lax.axis_index("dev")
    devices = groups * shards
    me = my_group * shards + my_shard
    per_old = tables.shape[1]
    tile_rows = tables.shape[2]
    local = groups * per_old
    slots = shards * capacity
    table_count, block_count = positions.shape
    look_rows = ids.shape[1]

    def prepare_source():
        number = iota((local, 1), 0)
        place = jnp.zeros((local, 1), jnp.int32)
        for base in range(0, block_count, SPAN):
            span = min(SPAN, block_count - base)
            old = base + iota((local, span), 1)
            counter = old // (per_old * shards) * per_old + old % per_old
            match = (old // per_old % shards == my_shard) & (counter == number)
            row = positions[pl.ds(my_group, 1), base : base + span]
            place += jnp.sum(jnp.where(match, row, 0), axis=1, keepdims=True)
        target = place // local
        lane, line = iota((local, local), 1), iota((local, local), 0)
        before = (target == as_row(target, local)) & (lane < line)
        slot_of = target * capacity + jnp.sum(jnp.where(before, 1, 0), axis=1, keepdims=True)
        slot = iota((local, source_words.shape[1]), 1)
        source_words[...] = jnp.sum(jnp.where(slot_of == slot, number, 0), axis=0, keepdims=True)
        copy = pltpu.make_async_copy(source_words, source_of, word_sem.at[0])
        copy.start()
        copy.wait()

    def prepare_picker():
        place = my_shard * local + iota((local, 1), 0)
        inverse = jnp.zeros((local, 1), jnp.int32)
        for base in range(0, block_count, SPAN):
            span = min(SPAN, block_count - base)
            old = base + iota((local, span), 1)
            row = positions[pl.ds(my_group, 1), base : base + span]
            inverse += jnp.sum(jnp.where(row == place, old, 0), axis=1, keepdims=True)
        source = inverse // per_old % shards
        rank = inverse // (per_old * shards) * per_old + inverse % per_old
        ahead = (as_row(source, local) == source) & (as_row(rank, local) < rank)
        pick = source * capacity + jnp.sum(jnp.where(ahead, 1, 0), axis=1, keepdims=True)
        picker_words[...] = as_row(pick, picker_words.shape[1])
        copy = pltpu.make_async_copy(picker_words, picker, word_sem.at[1])
        copy.start()
        copy.wait()

    def prepare_requests(index):
        wanted = as_column(ids[index : index + 1, :])
        block = wanted // tile_rows
        place = jnp.zeros((look_rows, 1), jnp.int32)
        for base in range(0, block_count, SPAN):
            span = min(SPAN, block_count - base)
            row = positions[index : index + 1, base : base + span]
            match = block == base + iota((look_rows, span), 1)
            place += jnp.sum(jnp.where(match, row, 0), axis=1, keepdims=True)
        owner = place // local
        local_row = place % local * tile_rows + wanted % tile_rows
        lane, line = iota((look_rows, look_rows), 1), iota((look_rows, look_rows), 0)
        before = (owner == as_row(owner, look_rows)) & (lane < line)
        turn = jnp.sum(jnp.where(before, 1, 0), axis=1, keepdims=True)
        seat = (index * shards + owner) * limit + turn
        final_words[index : index + 1, :] = as_row(seat, look_rows)

        def list_rows(shard, carry):
            match = (owner == shard) & (turn == iota((look_rows, asking.shape[2]), 1))
            asking[index * shards + shard] = jnp.sum(
                jnp.where(match, local_row, 0), axis=0, keepdims=True
            )
            return carry

        lax.fori_loop(0, shards, list_rows, 0)

    def coords(peer):
        return (peer // shards, peer % shards)

    def remote(src, dst, send_sem, recv_sem, device):
        return pltpu.make_async_remote_copy(
            src_ref=src,
            dst_ref=dst,
            send_sem=send_sem,
            recv_sem=recv_sem,
            device_id=device,
            device_id_type=MESH,
        )

    loads = []
    for index, (source, target) in enumerate(
        ((positions_hbm, positions), (ids_hbm, ids), (accum_hbm, accum))
    ):
        load = pltpu.make_async_copy(source, target, load_sem.at[index])
        load.start()
        loads.append(load)

    barrier = pltpu.get_barrier_semaphore()

    def greet(step, carry):
        pl.semaphore_signal(
            barrier, inc=1, device_id=coords((me + step) % devices), device_id_type=MESH
        )
        return carry

    lax.fori_loop(1, devices, greet, 0)
    for load in loads:
        load.wait()
    for index in range(table_count):
        for block in range(per_old):
            sums[index, block] = accum[index : index + 1, block * tile_rows : (block + 1) * tile_rows]
    prepare_source()
    pl.semaphore_wait(barrier, devices - 1)

    mine = pl.ds(my_group * per_old, per_old)
    own_copies = []
    for chunk in range(CHUNKS):
        rows = pl.ds(STARTS[chunk], PIECES[chunk])
        for step in range(1, groups):
            wanted = (my_group + step) % groups
            remote(
                tables.at[wanted, :, rows, :],
                held[chunk].at[mine],
                grp_send.at[chunk],
                grp_recv.at[chunk],
                (wanted, my_shard),
            ).start()
        own = pltpu.make_async_copy(
            tables.at[my_group, :, rows, :], held[chunk].at[mine], own_grp.at[chunk]
        )
        own.start()
        own_copies.append(own)
        if chunk == 0:
            for step in range(1, groups):
                wanted = (my_group + step) % groups
                remote(
                    sums.at[wanted],
                    held_sums.at[mine],
                    grp_send.at[CHUNKS],
                    grp_recv.at[CHUNKS],
                    (wanted, my_shard),
                ).start()
            own_sums_copy = pltpu.make_async_copy(
                sums.at[my_group], held_sums.at[mine], own_grp.at[CHUNKS]
            )
            own_sums_copy.start()

    order = sorted(range(1, shards), key=lambda step: abs(step - shards // 2))
    others = pl.ds(0, (groups - 1) * per_old)
    other_slots = pl.ds(0, (shards - 1) * capacity)
    own_dev_copies = []

    def exchange(send_ref, got_ref, index):
        for step in order:
            peer = (my_shard + step) % shards
            remote(
                send_ref.at[pl.ds(peer * capacity, capacity)],
                got_ref.at[pl.ds(my_shard * capacity, capacity)],
                dev_send.at[index],
                dev_recv.at[index],
                (my_group, peer),
            ).start()
        own = pltpu.make_async_copy(
            send_ref.at[pl.ds(my_shard * capacity, capacity)],
            got_ref.at[pl.ds(my_shard * capacity, capacity)],
            own_dev.at[index],
        )
        own.start()
        own_dev_copies.append(own)

    def send_requests():
        def ask(step, carry):
            peer = (me + step) % devices
            remote(
                asking.at[peer], asked.at[me], ask_sem.at[0], ask_sem.at[1], coords(peer)
            ).start()
            return carry

        lax.fori_loop(1, devices, ask, 0)
        own_ask = pltpu.make_async_copy(asking.at[me], asked.at[me], own_sem.at[0])
        own_ask.start()
        return own_ask

    for chunk in range(CHUNKS):
        own_copies[chunk].wait()
        remote(
            held[chunk].at[others],
            held[chunk].at[others],
            grp_send.at[chunk],
            grp_recv.at[chunk],
            (my_group, my_shard),
        ).wait_recv()

        def pack(slot, carry):
            send[chunk][slot] = held[chunk][source_of[0, slot]]
            return carry

        lax.fori_loop(0, slots, pack, 0, unroll=UNROLL)
        exchange(send[chunk], got[chunk], chunk)
        if chunk == 0:
            own_sums_copy.wait()
            remote(
                held_sums.at[others],
                held_sums.at[others],
                grp_send.at[CHUNKS],
                grp_recv.at[CHUNKS],
                (my_group, my_shard),
            ).wait_recv()

            def pack_sums(slot, carry):
                send_sums[slot] = held_sums[source_of[0, slot]]
                return carry

            lax.fori_loop(0, slots, pack_sums, 0)
            exchange(send_sums, got_sums, CHUNKS)
        if chunk < table_count:
            prepare_requests(chunk)
        if chunk == min(table_count, CHUNKS) - 1:
            for index in range(chunk + 1, table_count):
                prepare_requests(index)
            own_ask = send_requests()

    prepare_picker()
    final_copy = pltpu.make_async_copy(final_words, final, word_sem.at[2])
    final_copy.start()
    final_copy.wait()

    own_ask.wait()
    remote(
        asked.at[pl.ds(0, devices - 1)],
        asked.at[pl.ds(0, devices - 1)],
        ask_sem.at[0],
        ask_sem.at[1],
        (my_group, my_shard),
    ).wait_recv()
    to_scalar = pltpu.make_async_copy(asked, asked_scalar, own_sem.at[1])
    to_scalar.start()
    to_scalar.wait()

    def arrived(got_ref, index):
        own_dev_copies[index].wait()
        remote(
            got_ref.at[other_slots],
            got_ref.at[other_slots],
            dev_send.at[index],
            dev_recv.at[index],
            (my_group, my_shard),
        ).wait_recv()

    own_dev_copies[:] = [own_dev_copies[0]] + own_dev_copies[2:] + [own_dev_copies[1]]

    arrived(got_sums, CHUNKS)

    def place_sums(place, carry):
        new_sums[place] = got_sums[picker[0, place]]
        return carry

    lax.fori_loop(0, local, place_sums, 0)

    for chunk in range(CHUNKS):
        arrived(got[chunk], chunk)

        def place_rows(place, carry):
            start = pl.multiple_of(place * tile_rows + STARTS[chunk], 8)
            table[pl.ds(start, PIECES[chunk]), :] = got[chunk][picker[0, place]]
            return carry

        lax.fori_loop(0, local, place_rows, 0, unroll=UNROLL)

    def gather(peer):
        for at in range(limit):
            row = asked_scalar[peer, 0, at]
            answer[peer, at : at + 1, :] = table[pl.ds(row, 1), :]

    def reply(step, carry):
        turn = step // groups
        sign = turn % 2
        away = shards // 2 + sign * (turn + 1) // 2 - (1 - sign) * (turn // 2)
        group = (my_group + groups - 1 - step % groups) % groups
        shard = (my_shard + away) % shards
        peer = group * shards + shard
        gather(peer)
        remote(
            answer.at[peer],
            returned.at[pl.ds(me * limit, limit)],
            ans_sem.at[0],
            ans_sem.at[1],
            (group, shard),
        ).start()
        return carry

    lax.fori_loop(0, devices - 1, reply, 0)
    gather(me)
    own_answer = pltpu.make_async_copy(
        answer.at[me], returned.at[pl.ds(me * limit, limit)], own_sem.at[2]
    )
    own_answer.start()
    own_answer.wait()
    remote(
        returned.at[pl.ds(0, (devices - 1) * limit)],
        returned.at[pl.ds(0, (devices - 1) * limit)],
        ans_sem.at[0],
        ans_sem.at[1],
        (my_group, my_shard),
    ).wait_recv()

    batch = 16 // table_count

    def look(step, carry):
        for at in range(batch):
            for index in range(table_count):
                line = (step * batch + at) * table_count + index
                seat = final[index, step * batch + at]
                looked[pl.ds(line, 1), :] = returned[pl.ds(seat, 1), :]
        return carry

    lax.fori_loop(0, look_rows // batch, look, 0)

    for chunk in range(CHUNKS):
        remote(
            held[chunk].at[others],
            held[chunk].at[others],
            grp_send.at[chunk],
            grp_recv.at[chunk],
            (my_group, my_shard),
        ).wait_send()
        remote(
            send[chunk].at[other_slots],
            send[chunk].at[other_slots],
            dev_send.at[chunk],
            dev_recv.at[chunk],
            (my_group, my_shard),
        ).wait_send()
    remote(
        held_sums.at[others],
        held_sums.at[others],
        grp_send.at[CHUNKS],
        grp_recv.at[CHUNKS],
        (my_group, my_shard),
    ).wait_send()
    remote(
        send_sums.at[other_slots],
        send_sums.at[other_slots],
        dev_send.at[CHUNKS],
        dev_recv.at[CHUNKS],
        (my_group, my_shard),
    ).wait_send()
    for ref, sem, count in ((asked, ask_sem, 1), (returned, ans_sem, limit)):
        remote(
            ref.at[pl.ds(0, (devices - 1) * count)],
            ref.at[pl.ds(0, (devices - 1) * count)],
            sem.at[0],
            sem.at[1],
            (my_group, my_shard),
        ).wait_send()


def body(tables, accum, block_position, lookup_ids):
    groups = lax.axis_size("grp")
    shards = lax.axis_size("dev")
    table_count, old_rows, width = tables.shape
    per_old = old_rows // TILE
    local = groups * per_old
    longer = local // 2 + 1
    capacity = -(-longer // shards) + -(-(local - longer) // shards)
    look_rows = lookup_ids.shape[0]
    limit = 2 * look_rows // shards
    devices = groups * shards
    i32 = jnp.int32
    lanes = -(-limit // LANES) * LANES
    words = -(-shards * capacity // LANES) * LANES
    local_lanes = -(-local // LANES) * LANES
    f32 = jnp.float32
    vmem = pl.BlockSpec(memory_space=pltpu.VMEM)
    hbm = pl.BlockSpec(memory_space=pltpu.HBM)
    new_table, new_sums, looked = pl.pallas_call(
        functools.partial(kernel, groups, shards, capacity, limit),
        out_shape=(
            jax.ShapeDtypeStruct((local * TILE, width), f32),
            jax.ShapeDtypeStruct((local, 1, TILE), f32),
            jax.ShapeDtypeStruct((look_rows * table_count, width), f32),
        ),
        in_specs=[hbm, hbm, hbm, hbm],
        out_specs=(vmem, vmem, vmem),
        scratch_shapes=[pltpu.VMEM((local, piece, width), f32) for piece in PIECES]
        + [pltpu.VMEM((shards * capacity, piece, width), f32) for piece in PIECES + PIECES]
        + [
            pltpu.VMEM((local, 1, TILE), f32),
            pltpu.VMEM((shards * capacity, 1, TILE), f32),
            pltpu.VMEM((shards * capacity, 1, TILE), f32),
            pltpu.VMEM(block_position.shape, i32),
            pltpu.VMEM((table_count, look_rows), i32),
            pltpu.VMEM(accum.shape, f32),
            pltpu.VMEM((table_count, per_old, 1, TILE), f32),
            pltpu.VMEM((1, words), i32),
            pltpu.VMEM((1, local_lanes), i32),
            pltpu.VMEM((table_count, look_rows), i32),
            pltpu.SMEM((1, words), i32),
            pltpu.SMEM((1, local_lanes), i32),
            pltpu.SMEM((table_count, look_rows), i32),
            pltpu.VMEM((devices, 1, lanes), i32),
            pltpu.VMEM((devices, 1, lanes), i32),
            pltpu.SMEM((devices, 1, lanes), i32),
            pltpu.VMEM((devices, limit, width), f32),
            pltpu.VMEM((devices * limit, width), f32),
            pltpu.SemaphoreType.DMA((CHUNKS + 1,)),
            pltpu.SemaphoreType.DMA((CHUNKS + 1,)),
            pltpu.SemaphoreType.DMA((CHUNKS + 1,)),
            pltpu.SemaphoreType.DMA((CHUNKS + 1,)),
            pltpu.SemaphoreType.DMA((2,)),
            pltpu.SemaphoreType.DMA((2,)),
            pltpu.SemaphoreType.DMA((CHUNKS + 1,)),
            pltpu.SemaphoreType.DMA((CHUNKS + 1,)),
            pltpu.SemaphoreType.DMA((3,)),
            pltpu.SemaphoreType.DMA((3,)),
            pltpu.SemaphoreType.DMA((3,)),
        ],
        compiler_params=pltpu.CompilerParams(
            collective_id=0, has_side_effects=True, vmem_limit_bytes=32 * 1024 * 1024
        ),
    )(
        block_position,
        lookup_ids.T,
        tables.reshape(table_count, per_old, TILE, width),
        accum,
    )
    return (
        new_table.reshape(1, local * TILE, width),
        new_sums.reshape(1, local * TILE),
        looked.reshape(look_rows, table_count, width),
    )


def solution(mesh):
    placed = (P(None, ("grp", "dev"), None), P(None, ("grp", "dev")), P(), P(("grp", "dev"), None))
    return jax.shard_map(
        body,
        mesh=mesh,
        in_specs=placed,
        out_specs=(P("grp", "dev", None), P("grp", "dev"), P(("grp", "dev"), None, None)),
        check_vma=False,
    )
```
